32 devices in a mesh: group: 2 (over x), seq: 16 (over z, y, core).
Axes of the slice: x: 2, y: 2, z: 4, core: 2. Of those that a mesh axis runs over, the one named last changes fastest.
Arguments:
- queries: bfloat16 [8192, 768], P(('group', 'seq')), parts along dimension 0, may hold values from -6 to 6
- key_rows: bfloat16 [8192, 768], P(('group', 'seq')), parts along dimension 0, may hold values from -6 to 6
- value_rows: bfloat16 [8192, 768], P(('group', 'seq')), parts along dimension 0, may hold values from -20 to 20
- dilation: int32 [12], replicated, may hold values from 2 to 30, as said below
- global_rows: int32 [128], P('group'), parts along dimension 0, may hold values from 0 to 4095, as said below
- out_weight: bfloat16 [768, 1536], replicated, may hold values from -0.21875 to 0.21875
- mlp_up: bfloat16 [1536, 3072], P('seq'), may hold values from -0.15625 to 0.15625
- mlp_down: bfloat16 [3072, 1536], P('seq'), may hold values from -0.109375 to 0.109375
Outputs:
- attended: bfloat16 [8192, 1536], P(('group', 'seq')), parts along dimension 0
- mlp_out: bfloat16 [8192, 1536], P(('group', 'seq')), parts along dimension 0
The draws below stay inside these ranges and needn't reach their ends.
There are 2 independent parts, one for each index of `group`. The reference program is written for one: setup_inputs(seed, part) draws one part's arguments, and reference() takes and returns one part's arrays. A program takes and returns all parts, laid end to end along the dimension named above; an argument that names none is the same for every part. Nothing has to cross between parts.
Inputs may be any that keep to these rules, and one draw needn't show every extreme that they name: `dilation`: each offset is a multiple of 2; some head has the smallest and some the largest. `global_rows`: distinct positions.
All inputs are finite; a program needn't handle non-finite values.
Results may differ from the reference program's by a relative error of at most 0.0071.
Values may be sent and summed in bfloat16 or wider, within the bound.
A program may use at most 192 MiB of HBM per device.

```python
import jax
import jax.numpy as jnp
from jax import lax

D = 1536
H = 12
DH = 64
FF = 3072
BLK = 128
GLOBALS = 64
TOK_DEV = 256
HD = 768
LEN = 4096
N_SEQ = 16


def global_positions(key):
    return jax.random.permutation(jax.random.fold_in(key, 11), TOK_DEV * N_SEQ)[:GLOBALS].astype(jnp.int32)


def aligned_parts(key):
    length = TOK_DEV * N_SEQ
    positions = global_positions(key)
    is_global = jnp.zeros((length,), dtype=bool).at[positions].set(True)
    return is_global


def draw_queries(key, part):
    length = TOK_DEV * N_SEQ
    is_global = aligned_parts(key)
    base = jax.random.normal(jax.random.fold_in(key, 21), (length, H, DH))
    base = jnp.clip(jnp.where(is_global[:, None, None], 3.0 * base, base), -6.0, 6.0)
    return base.reshape(length, H * DH).astype(jnp.bfloat16)


def draw_key_rows(key, part):
    length = TOK_DEV * N_SEQ
    base = jnp.clip(jax.random.normal(jax.random.fold_in(key, 22), (length, H, DH)), -6.0, 6.0)
    return base.reshape(length, H * DH).astype(jnp.bfloat16)


def draw_dilation(key, part):
    offsets = jax.random.randint(jax.random.fold_in(key, 31), (H,), 1, N_SEQ)
    order = jax.random.permutation(jax.random.fold_in(key, 32), H)
    offsets = offsets.at[order[0]].set(1).at[order[1]].set(N_SEQ - 1)
    return (offsets * (TOK_DEV // BLK)).astype(jnp.int32)


def draw_global_rows(key, part):
    return global_positions(key)


def shard_levels(own_key, shape, shards, low, largest):
    factor_of, own = 1.0, jax.random.fold_in(own_key, 6)
    for axis_at, shards_of in shards:
        draws = jnp.exp(jax.random.uniform(jax.random.fold_in(own, axis_at), (shards_of,), jnp.float32, low / len(shards), largest / len(shards)))
        factor_of = factor_of * jnp.repeat(draws, shape[axis_at] // shards_of).reshape([-1 if axis == axis_at else 1 for axis in range(len(shape))])
    return factor_of


def centred(rng, shape, scale, most, cuts=(), kind=jnp.bfloat16):
    entries = jax.random.normal(rng, shape, jnp.float32) * scale
    if len(cuts) > 0:
        entries = shard_levels(rng, shape, cuts, -0.22, 0.18) * entries
    return jnp.clip(entries, min=-most, max=most).astype(kind)


def setup_inputs(seed: int = 0, part: int = 0) -> dict:
    streams_of = jax.random.split(jax.random.key(seed), 9)
    own_keys = jax.random.split(jax.random.fold_in(streams_of[8], part), 9)
    queries = draw_queries(jax.random.fold_in(jax.random.fold_in(streams_of[8], part), 71), part)
    key_rows = draw_key_rows(jax.random.fold_in(jax.random.fold_in(streams_of[8], part), 71), part)
    value_rows = centred(own_keys[2], (LEN, HD), 4.0, 20.0, ((0, 16),))
    dilation = draw_dilation(jax.random.fold_in(streams_of[8], 71), part)
    global_rows = draw_global_rows(jax.random.fold_in(jax.random.fold_in(streams_of[8], part), 71), part)
    out_weight = centred(streams_of[5], (HD, D), HD ** -0.5, 0.21875)
    mlp_up = centred(streams_of[6], (D, FF), D ** -0.5, 0.15625, ((0, 16),))
    mlp_down = centred(streams_of[7], (FF, D), FF ** -0.5, 0.109375, ((0, 16),))
    return dict(queries=queries, key_rows=key_rows, value_rows=value_rows, dilation=dilation, global_rows=global_rows, out_weight=out_weight, mlp_up=mlp_up, mlp_down=mlp_down)


def attend_blocks(query_blocks, local_keys, local_values, glob_keys, glob_values):
    count = query_blocks.shape[0]
    keys_all = jnp.concatenate([local_keys, jnp.broadcast_to(glob_keys[None], (count,) + glob_keys.shape)], axis=1).astype(jnp.float32)
    values_all = jnp.concatenate([local_values, jnp.broadcast_to(glob_values[None], (count,) + glob_values.shape)], axis=1).astype(jnp.float32)
    scores = jnp.einsum('nqhd,nkhd->nhqk', query_blocks.astype(jnp.float32), keys_all) * (DH ** -0.5)
    peak = jnp.max(scores, axis=-1, keepdims=True)
    exp_terms = jnp.exp(scores - peak)
    totals = jnp.sum(exp_terms, axis=-1, keepdims=True)
    weights = (exp_terms / totals).astype(jnp.bfloat16)
    return jnp.einsum('nhqk,nkhd->nqhd', weights.astype(jnp.float32), values_all)


def reference(queries, key_rows, value_rows, dilation, global_rows, out_weight, mlp_up, mlp_down):
    length = queries.shape[0]
    blocks = length // BLK
    per_dev = TOK_DEV // BLK
    query_blk = queries.reshape(blocks, BLK, H, DH)
    block_key_rows = key_rows.reshape(blocks, BLK, H, DH)
    block_value_rows = value_rows.reshape(blocks, BLK, H, DH)
    head_count = jnp.arange(H, dtype=jnp.int32)
    target_output = (jnp.arange(blocks, dtype=jnp.int32)[:, None] + dilation[None, :]) % blocks
    dilated_key_rows = block_key_rows[target_output, :, head_count[None, :], :].transpose(0, 2, 1, 3)
    dilated_value_rows = block_value_rows[target_output, :, head_count[None, :], :].transpose(0, 2, 1, 3)
    neighbour_key_rows = jnp.concatenate([jnp.roll(block_key_rows, 1, axis=0), block_key_rows, jnp.roll(block_key_rows, -1, axis=0), dilated_key_rows], axis=1)
    neighbour_value_rows = jnp.concatenate([jnp.roll(block_value_rows, 1, axis=0), block_value_rows, jnp.roll(block_value_rows, -1, axis=0), dilated_value_rows], axis=1)
    glob_query = queries[global_rows].reshape(GLOBALS, H, DH)
    glob_keys = key_rows[global_rows].reshape(GLOBALS, H, DH)
    glob_values = value_rows[global_rows].reshape(GLOBALS, H, DH)

    def per_device(items):
        return attend_blocks(items[0], items[1], items[2], glob_keys, glob_values)

    block_out = lax.map(per_device, (query_blk.reshape(N_SEQ, per_dev, BLK, H, DH),
                                     neighbour_key_rows.reshape(N_SEQ, per_dev, 4 * BLK, H, DH),
                                     neighbour_value_rows.reshape(N_SEQ, per_dev, 4 * BLK, H, DH)))
    attention = block_out.reshape(length, H * DH)

    key_heads = key_rows.astype(jnp.float32).reshape(length, H, DH).transpose(1, 0, 2)
    value_heads = value_rows.astype(jnp.float32).reshape(length, H, DH).transpose(1, 0, 2)
    query_heads = glob_query.astype(jnp.float32).transpose(1, 0, 2)

    def per_head(items):
        head_query, head_keys, head_values = items
        scores = jnp.dot(head_query, head_keys.T, precision=lax.Precision.HIGHEST) * (DH ** -0.5)
        peak = jnp.max(scores, axis=1, keepdims=True)
        exp_terms = jnp.exp(scores - peak)
        totals = jnp.sum(exp_terms, axis=1, keepdims=True)
        return jnp.dot(exp_terms, head_values, precision=lax.Precision.HIGHEST) / totals

    global_out = lax.map(per_head, (query_heads, key_heads, value_heads))
    global_out = global_out.transpose(1, 0, 2).reshape(GLOBALS, H * DH)
    attention = attention.at[global_rows].set(global_out).astype(jnp.bfloat16)
    attended = jnp.dot(attention, out_weight, preferred_element_type=jnp.float32).astype(jnp.bfloat16)

    def per_rows(rows):
        pre = jnp.dot(rows, mlp_up, preferred_element_type=jnp.float32)
        hidden = jax.nn.gelu(pre, approximate=True).astype(jnp.bfloat16)
        return jnp.dot(hidden, mlp_down, preferred_element_type=jnp.float32).astype(jnp.bfloat16)

    mlp_out = lax.map(per_rows, attended.reshape(N_SEQ, TOK_DEV, D)).reshape(length, D)
    return attended, mlp_out
```

```python
import functools

import jax
import jax.numpy as jnp
from jax import lax
from jax.experimental import pallas as pl
from jax.experimental.pallas import tpu as pltpu
from jax.sharding import PartitionSpec as P

H = 12
DH = 64
BLK = 128
GLOBALS = 64
LANES = 2 * DH
PAIRS = H // 2
CHUNK = 1024


def split_pair(rows):
    lane = lax.broadcasted_iota(jnp.int32, rows.shape, 1)
    zero = jnp.zeros_like(rows)
    return jnp.concatenate(
        [jnp.where(lane < DH, rows, zero), jnp.where(lane < DH, zero, rows)], axis=0
    )


def join_pair(first, second):
    lane = lax.broadcasted_iota(jnp.int32, first.shape, 1)
    return jnp.where(lane < DH, first, second)


def dot_t(left, right):
    return lax.dot_general(
        left, right, (((1,), (1,)), ((), ())), preferred_element_type=jnp.float32
    )


def dot(left, right):
    return jnp.dot(left, right, preferred_element_type=jnp.float32)


def attention_kernel(
    length, scal, q_ref, col_ref, row_ref, kc_ref, vc_ref, k_hbm, v_hbm, out_ref,
    loc_k, loc_v, dil_k, dil_v, gq, gk, gv, top, total, acc, sems,
):
    step = pl.program_id(0)
    tok = q_ref.shape[0]
    chunk = kc_ref.shape[0]
    me = scal[H]
    start = me * tok

    def copies():
        made = []
        spans = [
            (lax.rem(start + length - BLK, length), 0, BLK),
            (start, BLK, tok),
            (lax.rem(start + tok, length), BLK + tok, BLK),
        ]
        for hbm, loc, dil in ((k_hbm, loc_k, dil_k), (v_hbm, loc_v, dil_v)):
            for source, target, size in spans:
                rows = pl.ds(pl.multiple_of(source, BLK), size)
                made.append((hbm.at[rows, :], loc.at[pl.ds(target, size), :]))
            for head in range(H):
                source = lax.rem(start + scal[head] * BLK, length)
                rows = pl.ds(pl.multiple_of(source, BLK), tok)
                made.append((hbm.at[rows, pl.ds(head // 2 * LANES, LANES)], dil.at[head]))
        return [
            pltpu.make_async_copy(source, target, sems.at[at])
            for at, (source, target) in enumerate(made)
        ]

    @pl.when(step == 0)
    def _():
        for copy in copies():
            copy.start()
        mine = col_ref[...] - start == lax.broadcasted_iota(jnp.int32, (GLOBALS, tok), 1)
        picked = dot(mine.astype(jnp.bfloat16), q_ref[...]) * DH ** (-0.5)
        for pair in range(PAIRS):
            lanes = slice(pair * LANES, (pair + 1) * LANES)
            gq[pair] = split_pair(picked[:, lanes]).astype(jnp.bfloat16)
        gk[...] = jnp.zeros_like(gk)
        gv[...] = jnp.zeros_like(gv)
        top[...] = jnp.full_like(top, -1e30)
        total[...] = jnp.zeros_like(total)
        acc[...] = jnp.zeros_like(acc)

    here = col_ref[...] - step * chunk == lax.broadcasted_iota(jnp.int32, (GLOBALS, chunk), 1)
    here = here.astype(jnp.bfloat16)
    gk[...] += dot(here, kc_ref[...])
    gv[...] += dot(here, vc_ref[...])
    for pair in range(PAIRS):
        lanes = slice(pair * LANES, (pair + 1) * LANES)
        scores = dot_t(gq[pair], kc_ref[:, lanes])
        before = top[pair]
        peak = jnp.maximum(before, jnp.max(scores, axis=1, keepdims=True))
        scale = jnp.exp(before - peak)
        terms = jnp.exp(scores - peak)
        top[pair] = peak
        total[pair] = total[pair] * scale + jnp.sum(terms, axis=1, keepdims=True)
        acc[pair] = acc[pair] * scale + dot(terms.astype(jnp.bfloat16), vc_ref[:, lanes])

    @pl.when(step == pl.num_programs(0) - 1)
    def _():
        for copy in copies():
            copy.wait()
        mine = row_ref[...] - start == lax.broadcasted_iota(jnp.int32, (tok, GLOBALS), 0)
        owned = jnp.max(jnp.where(mine, 1.0, 0.0), axis=1, keepdims=True) > 0.5
        mine = mine.astype(jnp.bfloat16)
        for pair in range(PAIRS):
            lanes = slice(pair * LANES, (pair + 1) * LANES)
            ratio = acc[pair] / total[pair]
            placed = join_pair(ratio[:GLOBALS], ratio[GLOBALS:]).astype(jnp.bfloat16)
            placed = dot(mine, placed)
            far_k = join_pair(dil_k[2 * pair], dil_k[2 * pair + 1])
            far_v = join_pair(dil_v[2 * pair], dil_v[2 * pair + 1])
            glob_k = gk[:, lanes].astype(jnp.bfloat16)
            glob_v = gv[:, lanes].astype(jnp.bfloat16)
            for block in range(tok // BLK):
                rows = slice(block * BLK, (block + 1) * BLK)
                near = slice(block * BLK, (block + 3) * BLK)
                keys = jnp.concatenate([loc_k[near, lanes], far_k[rows], glob_k], axis=0)
                values = jnp.concatenate([loc_v[near, lanes], far_v[rows], glob_v], axis=0)
                scores = dot_t(split_pair(q_ref[rows, lanes]), keys) * DH ** (-0.5)
                terms = jnp.exp(scores - jnp.max(scores, axis=1, keepdims=True))
                weights = terms * (1.0 / jnp.sum(terms, axis=1, keepdims=True))
                mixed = dot(weights.astype(jnp.bfloat16), values)
                mixed = join_pair(mixed[:BLK], mixed[BLK:])
                out_ref[rows, lanes] = jnp.where(owned[rows], placed[rows], mixed).astype(
                    jnp.bfloat16
                )


def attention(queries, keys, values, dilation, global_rows):
    tok, width = queries.shape
    length = keys.shape[0]
    me = lax.axis_index("seq").astype(jnp.int32)
    scal = jnp.concatenate([dilation, me[None]])
    whole = lambda shape: pl.BlockSpec(shape, lambda i, s: (0, 0))
    chunked = pl.BlockSpec((CHUNK, width), lambda i, s: (i, 0))
    raw = pl.BlockSpec(memory_space=pl.ANY)
    far = pltpu.VMEM((H, tok, LANES), jnp.bfloat16)
    near = pltpu.VMEM((tok + 2 * BLK, width), jnp.bfloat16)
    state = pltpu.VMEM((PAIRS, 2 * GLOBALS, 1), jnp.float32)
    return pl.pallas_call(
        functools.partial(attention_kernel, length),
        out_shape=jax.ShapeDtypeStruct((tok, width), jnp.bfloat16),
        grid_spec=pltpu.PrefetchScalarGridSpec(
            num_scalar_prefetch=1,
            grid=(length // CHUNK,),
            in_specs=[
                whole((tok, width)), whole((GLOBALS, 1)), whole((1, GLOBALS)),
                chunked, chunked, raw, raw,
            ],
            out_specs=whole((tok, width)),
            scratch_shapes=[
                near, near, far, far,
                pltpu.VMEM((PAIRS, 2 * GLOBALS, LANES), jnp.bfloat16),
                pltpu.VMEM((GLOBALS, width), jnp.float32),
                pltpu.VMEM((GLOBALS, width), jnp.float32),
                state, state,
                pltpu.VMEM((PAIRS, 2 * GLOBALS, LANES), jnp.float32),
                pltpu.SemaphoreType.DMA((2 * (H + 3),)),
            ],
        ),
        compiler_params=pltpu.CompilerParams(vmem_limit_bytes=40 << 20),
        cost_estimate=pl.CostEstimate(
            flops=20_000_000_000, bytes_accessed=4 * length * width, transcendentals=5_000_000
        ),
    )(scal, queries, global_rows[:, None], global_rows[None, :], keys, values, keys, values)


def per_device(queries, key_rows, value_rows, dilation, global_rows, out_weight, mlp_up, mlp_down):
    keys = lax.all_gather(key_rows, "seq", axis=0, tiled=True)
    values = lax.all_gather(value_rows, "seq", axis=0, tiled=True)
    keys, values, mlp_up, mlp_down = lax.optimization_barrier((keys, values, mlp_up, mlp_down))
    up = lax.all_gather(mlp_up, "seq", axis=0, tiled=True)
    down = lax.all_gather(mlp_down, "seq", axis=0, tiled=True)
    mixed = attention(queries, keys, values, dilation, global_rows)
    attended = jnp.dot(mixed, out_weight, preferred_element_type=jnp.float32).astype(jnp.bfloat16)
    pre_act = jnp.dot(attended, up, preferred_element_type=jnp.float32)
    hidden = jax.nn.gelu(pre_act, approximate=True).astype(jnp.bfloat16)
    mlp_out = jnp.dot(hidden, down, preferred_element_type=jnp.float32).astype(jnp.bfloat16)
    return attended, mlp_out


def solution(mesh):
    rows = P(("group", "seq"), None)
    return jax.shard_map(
        per_device,
        mesh=mesh,
        in_specs=(rows, rows, rows, P(), P("group"), P(), P("seq", None), P("seq", None)),
        out_specs=(rows, rows),
        check_vma=False,
    )
```

```python
import functools

import jax
import jax.numpy as jnp
from jax import lax
from jax.experimental import pallas as pl
from jax.experimental.pallas import tpu as pltpu
from jax.sharding import PartitionSpec as P

H = 12
DH = 64
BLK = 128
GLOBALS = 64
LANES = 2 * DH
PAIRS = H // 2
CHUNK = 1024


def split_pair(rows):
    lane = lax.broadcasted_iota(jnp.int32, rows.shape, 1)
    zero = jnp.zeros_like(rows)
    return jnp.concatenate(
        [jnp.where(lane < DH, rows, zero), jnp.where(lane < DH, zero, rows)], axis=0
    )


def join_pair(first, second):
    lane = lax.broadcasted_iota(jnp.int32, first.shape, 1)
    return jnp.where(lane < DH, first, second)


def dot_t(left, right):
    return lax.dot_general(
        left, right, (((1,), (1,)), ((), ())), preferred_element_type=jnp.float32
    )


def dot(left, right):
    return jnp.dot(left, right, preferred_element_type=jnp.float32)


def attention_kernel(
    length, scal, q_ref, col_ref, row_ref, kc_ref, vc_ref, k_hbm, v_hbm, out_ref,
    loc_k, loc_v, dil_k, dil_v, gq, gk, gv, top, total, acc, sems,
):
    step = pl.program_id(0)
    tok = q_ref.shape[0]
    chunk = kc_ref.shape[0]
    me = scal[H]
    start = me * tok

    def copies():
        made = []
        spans = [
            (lax.rem(start + length - BLK, length), 0, BLK),
            (start, BLK, tok),
            (lax.rem(start + tok, length), BLK + tok, BLK),
        ]
        for hbm, loc, dil in ((k_hbm, loc_k, dil_k), (v_hbm, loc_v, dil_v)):
            for source, target, size in spans:
                rows = pl.ds(pl.multiple_of(source, BLK), size)
                made.append((hbm.at[rows, :], loc.at[pl.ds(target, size), :]))
            for head in range(H):
                source = lax.rem(start + scal[head] * BLK, length)
                rows = pl.ds(pl.multiple_of(source, BLK), tok)
                made.append((hbm.at[rows, pl.ds(head // 2 * LANES, LANES)], dil.at[head]))
        return [
            pltpu.make_async_copy(source, target, sems.at[at])
            for at, (source, target) in enumerate(made)
        ]

    @pl.when(step == 0)
    def _():
        for copy in copies():
            copy.start()
        mine = col_ref[...] - start == lax.broadcasted_iota(jnp.int32, (GLOBALS, tok), 1)
        picked = dot(mine.astype(jnp.bfloat16), q_ref[...]) * DH ** (-0.5)
        for pair in range(PAIRS):
            lanes = slice(pair * LANES, (pair + 1) * LANES)
            gq[pair] = split_pair(picked[:, lanes]).astype(jnp.bfloat16)
        gk[...] = jnp.zeros_like(gk)
        gv[...] = jnp.zeros_like(gv)
        top[...] = jnp.full_like(top, -1e30)
        total[...] = jnp.zeros_like(total)
        acc[...] = jnp.zeros_like(acc)

    here = col_ref[...] - step * chunk == lax.broadcasted_iota(jnp.int32, (GLOBALS, chunk), 1)
    here = here.astype(jnp.bfloat16)
    gk[...] += dot(here, kc_ref[...])
    gv[...] += dot(here, vc_ref[...])
    for pair in range(PAIRS):
        lanes = slice(pair * LANES, (pair + 1) * LANES)
        scores = dot_t(gq[pair], kc_ref[:, lanes])
        before = top[pair]
        peak = jnp.maximum(before, jnp.max(scores, axis=1, keepdims=True))
        scale = jnp.exp(before - peak)
        terms = jnp.exp(scores - peak)
        top[pair] = peak
        total[pair] = total[pair] * scale + jnp.sum(terms, axis=1, keepdims=True)
        acc[pair] = acc[pair] * scale + dot(terms.astype(jnp.bfloat16), vc_ref[:, lanes])

    @pl.when(step == pl.num_programs(0) - 1)
    def _():
        for copy in copies():
            copy.wait()
        mine = row_ref[...] - start == lax.broadcasted_iota(jnp.int32, (tok, GLOBALS), 0)
        owned = jnp.max(jnp.where(mine, 1.0, 0.0), axis=1, keepdims=True) > 0.5
        mine = mine.astype(jnp.bfloat16)
        for pair in range(PAIRS):
            lanes = slice(pair * LANES, (pair + 1) * LANES)
            ratio = acc[pair] / total[pair]
            placed = join_pair(ratio[:GLOBALS], ratio[GLOBALS:]).astype(jnp.bfloat16)
            placed = dot(mine, placed)
            far_k = join_pair(dil_k[2 * pair], dil_k[2 * pair + 1])
            far_v = join_pair(dil_v[2 * pair], dil_v[2 * pair + 1])
            glob_k = gk[:, lanes].astype(jnp.bfloat16)
            glob_v = gv[:, lanes].astype(jnp.bfloat16)
            for block in range(tok // BLK):
                rows = slice(block * BLK, (block + 1) * BLK)
                near = slice(block * BLK, (block + 3) * BLK)
                keys = jnp.concatenate([loc_k[near, lanes], far_k[rows], glob_k], axis=0)
                values = jnp.concatenate([loc_v[near, lanes], far_v[rows], glob_v], axis=0)
                scores = dot_t(split_pair(q_ref[rows, lanes]), keys) * DH ** (-0.5)
                terms = jnp.exp(scores - jnp.max(scores, axis=1, keepdims=True))
                weights = terms * (1.0 / jnp.sum(terms, axis=1, keepdims=True))
                mixed = dot(weights.astype(jnp.bfloat16), values)
                mixed = join_pair(mixed[:BLK], mixed[BLK:])
                out_ref[rows, lanes] = jnp.where(owned[rows], placed[rows], mixed).astype(
                    jnp.bfloat16
                )


def attention(queries, keys, values, dilation, global_rows):
    tok, width = queries.shape
    length = keys.shape[0]
    me = lax.axis_index("seq").astype(jnp.int32)
    scal = jnp.concatenate([dilation, me[None]])
    whole = lambda shape: pl.BlockSpec(shape, lambda i, s: (0, 0))
    chunked = pl.BlockSpec((CHUNK, width), lambda i, s: (i, 0))
    raw = pl.BlockSpec(memory_space=pl.ANY)
    far = pltpu.VMEM((H, tok, LANES), jnp.bfloat16)
    near = pltpu.VMEM((tok + 2 * BLK, width), jnp.bfloat16)
    state = pltpu.VMEM((PAIRS, 2 * GLOBALS, 1), jnp.float32)
    return pl.pallas_call(
        functools.partial(attention_kernel, length),
        out_shape=jax.ShapeDtypeStruct((tok, width), jnp.bfloat16),
        grid_spec=pltpu.PrefetchScalarGridSpec(
            num_scalar_prefetch=1,
            grid=(length // CHUNK,),
            in_specs=[
                whole((tok, width)), whole((GLOBALS, 1)), whole((1, GLOBALS)),
                chunked, chunked, raw, raw,
            ],
            out_specs=whole((tok, width)),
            scratch_shapes=[
                near, near, far, far,
                pltpu.VMEM((PAIRS, 2 * GLOBALS, LANES), jnp.bfloat16),
                pltpu.VMEM((GLOBALS, width), jnp.float32),
                pltpu.VMEM((GLOBALS, width), jnp.float32),
                state, state,
                pltpu.VMEM((PAIRS, 2 * GLOBALS, LANES), jnp.float32),
                pltpu.SemaphoreType.DMA((2 * (H + 3),)),
            ],
        ),
        compiler_params=pltpu.CompilerParams(vmem_limit_bytes=40 << 20),
        cost_estimate=pl.CostEstimate(
            flops=20_000_000_000, bytes_accessed=4 * length * width, transcendentals=5_000_000
        ),
    )(scal, queries, global_rows[:, None], global_rows[None, :], keys, values, keys, values)


MESH = pl.DeviceIdType.MESH


def gather_kernel(chips, *refs):
    ins, outs, sems = refs[:4], refs[4:8], refs[8:]
    ring_send, ring_recv, pair_send, pair_recv, core_send, core_recv, own_sems = sems
    half = chips // 2
    group, seq = lax.axis_index("group"), lax.axis_index("seq")
    role = group % 2
    chip, core = seq // 2, seq % 2
    odd = chip % 2
    pos = (1 - odd) * (chip // 2) + odd * (chips - 1 - chip // 2)

    def chip_at(place):
        place = (place + 2 * chips) % chips
        late = place // half
        return (1 - late) * 2 * place + late * (2 * (chips - 1 - place) + 1)

    ahead = (group, chip_at(pos + 1) * 2 + core)
    behind = (group, chip_at(pos - 1) * 2 + core)
    beside = (group, chip * 2 + 1 - core)
    across = (group + 1 - 2 * role, seq)

    barrier = pltpu.get_barrier_semaphore()
    for other in (ahead, behind, beside, across):
        pl.semaphore_signal(barrier, inc=1, device_id=other, device_id_type=MESH)
    pl.semaphore_wait(barrier, 4)

    def columns(at, side, part):
        width = ins[at].shape[1]
        first = 0
        if at < 2 and side is not None:
            width = width // 2
            first = side * width
        if part is not None:
            width = width // 2
            first = first + part * width
        if isinstance(first, int):
            return pl.ds(first, width)
        return pl.ds(pl.multiple_of(first, 128), width)

    def held(at, place, side, part):
        rows = ins[at].shape[0]
        first = (chip_at(place) * 2 + core) * rows
        return outs[at].at[pl.ds(pl.multiple_of(first, 8), rows), columns(at, side, part)]

    def twin(at, place, side, part):
        rows = ins[at].shape[0]
        first = (chip_at(place) * 2 + 1 - core) * rows
        return outs[at].at[pl.ds(pl.multiple_of(first, 8), rows), columns(at, side, part)]

    def part_of(way, hop):
        return way if hop == half else None

    def sign(way):
        return 1 - 2 * way

    def remote(source, target, send, recv, other):
        return pltpu.make_async_remote_copy(
            src_ref=source, dst_ref=target, send_sem=send, recv_sem=recv,
            device_id=other, device_id_type=MESH,
        )

    sent = []

    def ring(at, way, hop):
        index = (at * 2 + way) * half + hop - 1
        return ring_send.at[index], ring_recv.at[index], (ahead, behind)[way]

    def ring_start(at, way, hop):
        place, part = pos - sign(way) * (hop - 1), part_of(way, hop)
        target = held(at, place, role, part)
        source = ins[at].at[:, columns(at, role, part)] if hop == 1 else target
        copy = remote(source, target, *ring(at, way, hop))
        copy.start()
        sent.append(copy)

    def ring_wait(at, way, hop):
        here = held(at, pos - sign(way) * hop, role, part_of(way, hop))
        remote(here, here, *ring(at, way, hop)).wait_recv()

    def pair(at, way, hop):
        index = (at * 2 + way) * half + hop - 1
        return pair_send.at[index], pair_recv.at[index], across

    def pair_start(at, way, hop):
        here = held(at, pos - sign(way) * hop, role, part_of(way, hop))
        copy = remote(here, here, *pair(at, way, hop))
        copy.start()
        sent.append(copy)

    def pair_wait(at, way, hop):
        here = held(at, pos - sign(way) * hop, 1 - role, part_of(way, hop))
        remote(here, here, *pair(at, way, hop)).wait_recv()

    passed = []

    def core_start(at, place, side, part, source=None):
        index = len(passed)
        target = held(at, place, side, part)
        copy = remote(
            target if source is None else source, target,
            core_send.at[index], core_recv.at[index], beside,
        )
        copy.start()
        sent.append(copy)
        passed.append((at, place, side, part))

    own = []
    for at in range(4):
        for way in range(2):
            ring_start(at, way, 1)
    for at in range(4):
        core_start(at, pos, None, None, ins[at])
        copy = pltpu.make_async_copy(ins[at], held(at, pos, None, None), own_sems.at[at])
        copy.start()
        own.append(copy)
    for hop in range(1, half + 2):
        if hop <= half:
            for at in range(4):
                for way in range(2):
                    ring_wait(at, way, hop)
                    if hop < half:
                        ring_start(at, way, hop + 1)
                    if at < 2:
                        pair_start(at, way, hop)
                    core_start(at, pos - sign(way) * hop, role, part_of(way, hop))
        if hop > 1:
            for at in range(2):
                for way in range(2):
                    pair_wait(at, way, hop - 1)
                    core_start(at, pos - sign(way) * (hop - 1), 1 - role, part_of(way, hop - 1))
    for index, (at, place, side, part) in enumerate(passed):
        here = twin(at, place, side, part)
        remote(here, here, core_send.at[index], core_recv.at[index], beside).wait_recv()
    for copy in sent:
        copy.wait_send()
    for copy in own:
        copy.wait()


def gathered(arrays):
    devices = lax.axis_size("seq")
    chips = devices // 2
    half = chips // 2
    raw = pl.BlockSpec(memory_space=pl.ANY)
    dma = pltpu.SemaphoreType.DMA
    return pl.pallas_call(
        functools.partial(gather_kernel, chips),
        out_shape=[
            jax.ShapeDtypeStruct((a.shape[0] * devices, a.shape[1]), a.dtype) for a in arrays
        ],
        in_specs=[raw] * 4,
        out_specs=[raw] * 4,
        scratch_shapes=[
            dma((8 * half,)), dma((8 * half,)), dma((4 * half,)), dma((4 * half,)),
            dma((4 + 12 * half,)), dma((4 + 12 * half,)), dma((4,)),
        ],
        compiler_params=pltpu.CompilerParams(collective_id=0, has_side_effects=True),
    )(*arrays)


def per_device(queries, key_rows, value_rows, dilation, global_rows, out_weight, mlp_up, mlp_down):
    up, down, keys, values = gathered((mlp_up, mlp_down, key_rows, value_rows))
    mixed = attention(queries, keys, values, dilation, global_rows)
    attended = jnp.dot(mixed, out_weight, preferred_element_type=jnp.float32).astype(jnp.bfloat16)
    pre_act = jnp.dot(attended, up, preferred_element_type=jnp.float32)
    hidden = jax.nn.gelu(pre_act, approximate=True).astype(jnp.bfloat16)
    mlp_out = jnp.dot(hidden, down, preferred_element_type=jnp.float32).astype(jnp.bfloat16)
    return attended, mlp_out


def solution(mesh):
    rows = P(("group", "seq"), None)
    return jax.shard_map(
        per_device,
        mesh=mesh,
        in_specs=(rows, rows, rows, P(), P("group"), P(), P("seq", None), P("seq", None)),
        out_specs=(rows, rows),
        check_vma=False,
    )
```

```python
import functools

import jax
import jax.numpy as jnp
from jax import lax
from jax.experimental import pallas as pl
from jax.experimental.pallas import tpu as pltpu
from jax.sharding import PartitionSpec as P

H = 12
DH = 64
BLK = 128
GLOBALS = 64
LANES = 2 * DH
PAIRS = H // 2
CHUNK = 1024
SLOTS = 16
TILE = 16


def split_pair(rows):
    lane = lax.broadcasted_iota(jnp.int32, rows.shape, 1)
    zero = jnp.zeros_like(rows)
    return jnp.concatenate(
        [jnp.where(lane < DH, rows, zero), jnp.where(lane < DH, zero, rows)], axis=0
    )


def join_pair(first, second):
    lane = lax.broadcasted_iota(jnp.int32, first.shape, 1)
    return jnp.where(lane < DH, first, second)


def dot_t(left, right):
    return lax.dot_general(
        left, right, (((1,), (1,)), ((), ())), preferred_element_type=jnp.float32
    )


def dot(left, right):
    return jnp.dot(left, right, preferred_element_type=jnp.float32)


def head_mask(shape):
    row = lax.broadcasted_iota(jnp.int32, shape, 0) // SLOTS
    lane = lax.broadcasted_iota(jnp.int32, shape, 1) // DH
    return row == lane


def attention_kernel(
    length, scal, q_ref, col_ref, row_ref, kc_ref, vc_ref, k_hbm, v_hbm, out_ref,
    loc_k, loc_v, dil_k, dil_v, tile_k, tile_v, gq, top, total, acc, sems,
):
    step = pl.program_id(0)
    tok, width = q_ref.shape
    me, count = scal[H], scal[H + 1]
    start = me * tok

    def copies():
        made = []
        spans = [
            (lax.rem(start + length - BLK, length), 0, BLK),
            (start, BLK, tok),
            (lax.rem(start + tok, length), BLK + tok, BLK),
        ]
        for hbm, loc, dil in ((k_hbm, loc_k, dil_k), (v_hbm, loc_v, dil_v)):
            for source, target, size in spans:
                rows = pl.ds(pl.multiple_of(source, BLK), size)
                made.append((hbm.at[rows, :], loc.at[pl.ds(target, size), :]))
            for head in range(H):
                source = lax.rem(start + scal[head] * BLK, length)
                rows = pl.ds(pl.multiple_of(source, BLK), tok)
                made.append((hbm.at[rows, pl.ds(head // 2 * LANES, LANES)], dil.at[head]))
        return [
            pltpu.make_async_copy(source, target, sems.at[at])
            for at, (source, target) in enumerate(made)
        ]

    def slots():
        rows, cols = row_ref[...] - start, col_ref[...] - start
        row_own = jnp.where((rows >= 0) & (rows < tok), 1.0, 0.0)
        col_own = jnp.where((cols >= 0) & (cols < tok), 1.0, 0.0)
        square = (GLOBALS, GLOBALS)
        down = lax.broadcasted_iota(jnp.int32, square, 0)
        right = lax.broadcasted_iota(jnp.int32, square, 1)
        return rows, cols, row_own, col_own, down, right

    def picker_rows(group):
        rows, cols, row_own, col_own, down, right = slots()
        rank = jnp.sum(jnp.where(down < right, col_own, 0.0), axis=0, keepdims=True)
        rank = jnp.where(row_own > 0.5, rank, -1.0).astype(jnp.int32)
        slot = lax.broadcasted_iota(jnp.int32, (H * SLOTS, GLOBALS), 0) % SLOTS
        holds = jnp.where(slot + group * SLOTS == rank, 1.0, 0.0).astype(jnp.bfloat16)
        at = jnp.where(
            cols == lax.broadcasted_iota(jnp.int32, (GLOBALS, tok), 1), 1.0, 0.0
        ).astype(jnp.bfloat16)
        return dot(holds, at).astype(jnp.bfloat16)

    def picker_cols(group):
        rows, cols, row_own, col_own, down, right = slots()
        rank = jnp.sum(jnp.where(right < down, row_own, 0.0), axis=1, keepdims=True)
        rank = jnp.where(col_own > 0.5, rank, -1.0).astype(jnp.int32)
        slot = lax.broadcasted_iota(jnp.int32, (GLOBALS, H * SLOTS), 1) % SLOTS
        holds = jnp.where(slot + group * SLOTS == rank, 1.0, 0.0).astype(jnp.bfloat16)
        at = jnp.where(
            rows == lax.broadcasted_iota(jnp.int32, (tok, GLOBALS), 0), 1.0, 0.0
        ).astype(jnp.bfloat16)
        return dot(at, holds).astype(jnp.bfloat16)

    @pl.when(step == 0)
    def _():
        for copy in copies():
            copy.start()

        @pl.loop(0, GLOBALS)
        def _(at):
            source = pl.ds(pl.multiple_of(scal[H + 2 + at] // TILE * TILE, TILE), TILE)
            target = pl.ds(pl.multiple_of(at * TILE, TILE), TILE)
            for index, (hbm, tile) in enumerate(((k_hbm, tile_k), (v_hbm, tile_v))):
                pltpu.make_async_copy(
                    hbm.at[source, :], tile.at[target, :], sems.at[2 * (H + 3) + index]
                ).start()

        for group in range(GLOBALS // SLOTS):

            @pl.when(count > group * SLOTS)
            def _():
                picked = dot(picker_rows(group), q_ref[...]) * DH ** (-0.5)
                picked = jnp.where(head_mask(picked.shape), picked, 0.0)
                gq[group] = picked.astype(jnp.bfloat16)
                top[group] = jnp.full(top.shape[1:], -1e30, jnp.float32)
                total[group] = jnp.zeros(total.shape[1:], jnp.float32)
                acc[group] = jnp.zeros(acc.shape[1:], jnp.float32)

    for group in range(GLOBALS // SLOTS):

        @pl.when(count > group * SLOTS)
        def _():
            scores = dot_t(gq[group], kc_ref[...])
            before = top[group]
            peak = jnp.maximum(before, jnp.max(scores, axis=1, keepdims=True))
            scale = jnp.exp(before - peak)
            terms = jnp.exp(scores - peak)
            top[group] = peak
            total[group] = total[group] * scale + jnp.sum(terms, axis=1, keepdims=True)
            acc[group] = acc[group] * scale + dot(terms.astype(jnp.bfloat16), vc_ref[...])

    @pl.when(step == pl.num_programs(0) - 1)
    def _():
        for copy in copies():
            copy.wait()
        for index, (hbm, tile) in enumerate(((k_hbm, tile_k), (v_hbm, tile_v))):
            pltpu.make_async_copy(
                hbm.at[pl.ds(0, GLOBALS * TILE), :], tile, sems.at[2 * (H + 3) + index]
            ).wait()
        spot = lax.broadcasted_iota(jnp.int32, (GLOBALS, GLOBALS * TILE), 1)
        want = lax.broadcasted_iota(jnp.int32, (GLOBALS, GLOBALS * TILE), 0) * TILE
        here = jnp.where(spot == want + col_ref[...] % TILE, 1.0, 0.0).astype(jnp.bfloat16)
        for pair in range(PAIRS):
            lanes = slice(pair * LANES, (pair + 1) * LANES)
            far_k = join_pair(dil_k[2 * pair], dil_k[2 * pair + 1])
            far_v = join_pair(dil_v[2 * pair], dil_v[2 * pair + 1])
            glob_k = dot(here, tile_k[:, lanes]).astype(jnp.bfloat16)
            glob_v = dot(here, tile_v[:, lanes]).astype(jnp.bfloat16)
            for block in range(tok // BLK):
                rows = slice(block * BLK, (block + 1) * BLK)
                near = slice(block * BLK, (block + 3) * BLK)
                keys = jnp.concatenate([loc_k[near, lanes], far_k[rows], glob_k], axis=0)
                values = jnp.concatenate([loc_v[near, lanes], far_v[rows], glob_v], axis=0)
                scores = dot_t(split_pair(q_ref[rows, lanes]), keys) * DH ** (-0.5)
                terms = jnp.exp(scores - jnp.max(scores, axis=1, keepdims=True))
                weights = terms * (1.0 / jnp.sum(terms, axis=1, keepdims=True))
                mixed = dot(weights.astype(jnp.bfloat16), values)
                mixed = join_pair(mixed[:BLK], mixed[BLK:])
                out_ref[rows, lanes] = mixed.astype(jnp.bfloat16)

        for group in range(GLOBALS // SLOTS):

            @pl.when(count > group * SLOTS)
            def _():
                ratio = acc[group] / total[group]
                ratio = jnp.where(head_mask(ratio.shape), ratio, 0.0).astype(jnp.bfloat16)
                mine = picker_cols(group)
                placed = dot(mine, ratio).astype(jnp.bfloat16)
                owned = jnp.max(mine.astype(jnp.float32), axis=1, keepdims=True) > 0.5
                out_ref[...] = jnp.where(owned, placed, out_ref[...])


def attention(queries, keys, values, dilation, global_rows):
    tok, width = queries.shape
    length = keys.shape[0]
    groups = GLOBALS // SLOTS
    me = lax.axis_index("seq").astype(jnp.int32)
    count = jnp.sum((global_rows // tok == me).astype(jnp.int32))
    scal = jnp.concatenate([dilation, me[None], count[None], global_rows])
    whole = lambda shape: pl.BlockSpec(shape, lambda i, s: (0, 0))
    chunked = pl.BlockSpec((CHUNK, width), lambda i, s: (i, 0))
    raw = pl.BlockSpec(memory_space=pl.ANY)
    far = pltpu.VMEM((H, tok, LANES), jnp.bfloat16)
    near = pltpu.VMEM((tok + 2 * BLK, width), jnp.bfloat16)
    tile = pltpu.VMEM((GLOBALS * TILE, width), jnp.bfloat16)
    state = pltpu.VMEM((groups, H * SLOTS, 1), jnp.float32)
    return pl.pallas_call(
        functools.partial(attention_kernel, length),
        out_shape=jax.ShapeDtypeStruct((tok, width), jnp.bfloat16),
        grid_spec=pltpu.PrefetchScalarGridSpec(
            num_scalar_prefetch=1,
            grid=(length // CHUNK,),
            in_specs=[
                whole((tok, width)), whole((GLOBALS, 1)), whole((1, GLOBALS)),
                chunked, chunked, raw, raw,
            ],
            out_specs=whole((tok, width)),
            scratch_shapes=[
                near, near, far, far, tile, tile,
                pltpu.VMEM((groups, H * SLOTS, width), jnp.bfloat16),
                state, state,
                pltpu.VMEM((groups, H * SLOTS, width), jnp.float32),
                pltpu.SemaphoreType.DMA((2 * (H + 3) + 2,)),
            ],
        ),
        compiler_params=pltpu.CompilerParams(vmem_limit_bytes=58 << 20),
        cost_estimate=pl.CostEstimate(
            flops=20_000_000_000, bytes_accessed=4 * length * width, transcendentals=5_000_000
        ),
    )(scal, queries, global_rows[:, None], global_rows[None, :], keys, values, keys, values)


MESH = pl.DeviceIdType.MESH


def gather_kernel(chips, *refs):
    ins, outs, sems = refs[:4], refs[4:8], refs[8:]
    ring_send, ring_recv, pair_send, pair_recv, core_send, core_recv, own_sems = sems
    half = chips // 2
    group, seq = lax.axis_index("group"), lax.axis_index("seq")
    role = group % 2
    chip, core = seq // 2, seq % 2
    odd = chip % 2
    pos = (1 - odd) * (chip // 2) + odd * (chips - 1 - chip // 2)

    def chip_at(place):
        place = (place + 2 * chips) % chips
        late = place // half
        return (1 - late) * 2 * place + late * (2 * (chips - 1 - place) + 1)

    ahead = (group, chip_at(pos + 1) * 2 + core)
    behind = (group, chip_at(pos - 1) * 2 + core)
    beside = (group, chip * 2 + 1 - core)
    across = (group + 1 - 2 * role, seq)

    barrier = pltpu.get_barrier_semaphore()
    for other in (ahead, behind, beside, across):
        pl.semaphore_signal(barrier, inc=1, device_id=other, device_id_type=MESH)
    pl.semaphore_wait(barrier, 4)

    def columns(at, side, part):
        width = ins[at].shape[1]
        first = 0
        if at < 2 and side is not None:
            width = width // 2
            first = side * width
        if part is not None:
            width = width // 2
            first = first + part * width
        if isinstance(first, int):
            return pl.ds(first, width)
        return pl.ds(pl.multiple_of(first, 128), width)

    def held(at, place, side, part):
        rows = ins[at].shape[0]
        first = (chip_at(place) * 2 + core) * rows
        return outs[at].at[pl.ds(pl.multiple_of(first, 8), rows), columns(at, side, part)]

    def twin(at, place, side, part):
        rows = ins[at].shape[0]
        first = (chip_at(place) * 2 + 1 - core) * rows
        return outs[at].at[pl.ds(pl.multiple_of(first, 8), rows), columns(at, side, part)]

    def part_of(way, hop):
        return way if hop == half else None

    def sign(way):
        return 1 - 2 * way

    def remote(source, target, send, recv, other):
        return pltpu.make_async_remote_copy(
            src_ref=source, dst_ref=target, send_sem=send, recv_sem=recv,
            device_id=other, device_id_type=MESH,
        )

    sent = []

    def ring(at, way, hop):
        index = (at * 2 + way) * half + hop - 1
        return ring_send.at[index], ring_recv.at[index], (ahead, behind)[way]

    def ring_start(at, way, hop):
        place, part = pos - sign(way) * (hop - 1), part_of(way, hop)
        target = held(at, place, role, part)
        source = ins[at].at[:, columns(at, role, part)] if hop == 1 else target
        copy = remote(source, target, *ring(at, way, hop))
        copy.start()
        sent.append(copy)

    def ring_wait(at, way, hop):
        here = held(at, pos - sign(way) * hop, role, part_of(way, hop))
        remote(here, here, *ring(at, way, hop)).wait_recv()

    def pair(at, way, hop):
        index = (at * 2 + way) * half + hop - 1
        return pair_send.at[index], pair_recv.at[index], across

    def pair_start(at, way, hop):
        here = held(at, pos - sign(way) * hop, role, part_of(way, hop))
        copy = remote(here, here, *pair(at, way, hop))
        copy.start()
        sent.append(copy)

    def pair_wait(at, way, hop):
        here = held(at, pos - sign(way) * hop, 1 - role, part_of(way, hop))
        remote(here, here, *pair(at, way, hop)).wait_recv()

    passed = []

    def core_start(at, place, side, part, source=None):
        index = len(passed)
        target = held(at, place, side, part)
        copy = remote(
            target if source is None else source, target,
            core_send.at[index], core_recv.at[index], beside,
        )
        copy.start()
        sent.append(copy)
        passed.append((at, place, side, part))

    own = []
    for at in (0, 1):
        for way in range(2):
            ring_start(at, way, 1)
    for at in (2, 3):
        for way in range(2):
            ring_start(at, way, 1)
    for at in range(4):
        core_start(at, pos, None, None, ins[at])
        copy = pltpu.make_async_copy(ins[at], held(at, pos, None, None), own_sems.at[at])
        copy.start()
        own.append(copy)

    def ring_step(at, hop):
        for way in range(2):
            ring_wait(at, way, hop)
            if hop < half:
                ring_start(at, way, hop + 1)
            if at < 2:
                pair_start(at, way, hop)
            core_start(at, pos - sign(way) * hop, role, part_of(way, hop))

    for hop in range(1, half + 2):
        if hop <= half:
            ring_step(0, hop)
            ring_step(1, hop)
        if hop > 1:
            ring_step(2, hop - 1)
            ring_step(3, hop - 1)
            for at in range(2):
                for way in range(2):
                    pair_wait(at, way, hop - 1)
                    core_start(at, pos - sign(way) * (hop - 1), 1 - role, part_of(way, hop - 1))
    for index, (at, place, side, part) in enumerate(passed):
        here = twin(at, place, side, part)
        remote(here, here, core_send.at[index], core_recv.at[index], beside).wait_recv()
    for copy in sent:
        copy.wait_send()
    for copy in own:
        copy.wait()


def gathered(arrays):
    devices = lax.axis_size("seq")
    chips = devices // 2
    half = chips // 2
    raw = pl.BlockSpec(memory_space=pl.ANY)
    dma = pltpu.SemaphoreType.DMA
    return pl.pallas_call(
        functools.partial(gather_kernel, chips),
        out_shape=[
            jax.ShapeDtypeStruct((a.shape[0] * devices, a.shape[1]), a.dtype) for a in arrays
        ],
        in_specs=[raw] * 4,
        out_specs=[raw] * 4,
        scratch_shapes=[
            dma((8 * half,)), dma((8 * half,)), dma((4 * half,)), dma((4 * half,)),
            dma((4 + 12 * half,)), dma((4 + 12 * half,)), dma((4,)),
        ],
        compiler_params=pltpu.CompilerParams(collective_id=0, has_side_effects=True),
    )(*arrays)


def per_device(queries, key_rows, value_rows, dilation, global_rows, out_weight, mlp_up, mlp_down):
    up, down, keys, values = gathered((mlp_up, mlp_down, key_rows, value_rows))
    mixed = attention(queries, keys, values, dilation, global_rows)
    attended = jnp.dot(mixed, out_weight, preferred_element_type=jnp.float32).astype(jnp.bfloat16)
    pre_act = jnp.dot(attended, up, preferred_element_type=jnp.float32)
    hidden = jax.nn.gelu(pre_act, approximate=True).astype(jnp.bfloat16)
    mlp_out = jnp.dot(hidden, down, preferred_element_type=jnp.float32).astype(jnp.bfloat16)
    return attended, mlp_out


def solution(mesh):
    rows = P(("group", "seq"), None)
    return jax.shard_map(
        per_device,
        mesh=mesh,
        in_specs=(rows, rows, rows, P(), P("group"), P(), P("seq", None), P("seq", None)),
        out_specs=(rows, rows),
        check_vma=False,
    )
```

```python
import functools

import jax
import jax.numpy as jnp
from jax import lax
from jax.experimental import pallas as pl
from jax.experimental.pallas import tpu as pltpu
from jax.sharding import PartitionSpec as P

H = 12
DH = 64
BLK = 128
GLOBALS = 64
LANES = 2 * DH
PAIRS = H // 2
CHUNK = 1024
SLOTS = 16
TILE = 16


def split_pair(rows):
    lane = lax.broadcasted_iota(jnp.int32, rows.shape, 1)
    zero = jnp.zeros_like(rows)
    return jnp.concatenate(
        [jnp.where(lane < DH, rows, zero), jnp.where(lane < DH, zero, rows)], axis=0
    )


def join_pair(first, second):
    lane = lax.broadcasted_iota(jnp.int32, first.shape, 1)
    return jnp.where(lane < DH, first, second)


def dot_t(left, right):
    return lax.dot_general(
        left, right, (((1,), (1,)), ((), ())), preferred_element_type=jnp.float32
    )


def dot(left, right):
    return jnp.dot(left, right, preferred_element_type=jnp.float32)


def head_mask(shape):
    row = lax.broadcasted_iota(jnp.int32, shape, 0) // SLOTS
    lane = lax.broadcasted_iota(jnp.int32, shape, 1) // DH
    return row == lane


def attention_kernel(
    length, dilation, spots, q_ref, row_ref, kc_ref, vc_ref, k_hbm, v_hbm, out_ref,
    loc_k, loc_v, dil_k, dil_v, tile_k, tile_v, gq, top, total, acc, owns, sems,
):
    step = pl.program_id(0)
    tok, width = q_ref.shape
    me = lax.axis_index("seq")
    start = me * tok

    def copies():
        made = []
        spans = [
            (lax.rem(start + length - BLK, length), 0, BLK),
            (start, BLK, tok),
            (lax.rem(start + tok, length), BLK + tok, BLK),
        ]
        for hbm, loc, dil in ((k_hbm, loc_k, dil_k), (v_hbm, loc_v, dil_v)):
            for source, target, size in spans:
                rows = pl.ds(pl.multiple_of(source, BLK), size)
                made.append((hbm.at[rows, :], loc.at[pl.ds(target, size), :]))
            for head in range(H):
                source = lax.rem(start + dilation[head] * BLK, length)
                rows = pl.ds(pl.multiple_of(source, BLK), tok)
                made.append((hbm.at[rows, pl.ds(head // 2 * LANES, LANES)], dil.at[head]))
        return [
            pltpu.make_async_copy(source, target, sems.at[at])
            for at, (source, target) in enumerate(made)
        ]

    def column():
        square = (GLOBALS, GLOBALS)
        down = lax.broadcasted_iota(jnp.int32, square, 0)
        right = lax.broadcasted_iota(jnp.int32, square, 1)
        spread = jnp.where(down == right, row_ref[...].astype(jnp.float32), 0.0)
        return jnp.sum(spread, axis=1, keepdims=True).astype(jnp.int32)

    def slots():
        rows, cols = row_ref[...] - start, column() - start
        row_own = jnp.where((rows >= 0) & (rows < tok), 1.0, 0.0)
        col_own = jnp.where((cols >= 0) & (cols < tok), 1.0, 0.0)
        square = (GLOBALS, GLOBALS)
        down = lax.broadcasted_iota(jnp.int32, square, 0)
        right = lax.broadcasted_iota(jnp.int32, square, 1)
        return rows, cols, row_own, col_own, down, right

    def picker_rows(group):
        rows, cols, row_own, col_own, down, right = slots()
        rank = jnp.sum(jnp.where(down < right, col_own, 0.0), axis=0, keepdims=True)
        rank = jnp.where(row_own > 0.5, rank, -1.0).astype(jnp.int32)
        slot = lax.broadcasted_iota(jnp.int32, (H * SLOTS, GLOBALS), 0) % SLOTS
        holds = jnp.where(slot + group * SLOTS == rank, 1.0, 0.0).astype(jnp.bfloat16)
        at = jnp.where(
            cols == lax.broadcasted_iota(jnp.int32, (GLOBALS, tok), 1), 1.0, 0.0
        ).astype(jnp.bfloat16)
        return dot(holds, at).astype(jnp.bfloat16)

    def picker_cols(group):
        rows, cols, row_own, col_own, down, right = slots()
        rank = jnp.sum(jnp.where(right < down, row_own, 0.0), axis=1, keepdims=True)
        rank = jnp.where(col_own > 0.5, rank, -1.0).astype(jnp.int32)
        slot = lax.broadcasted_iota(jnp.int32, (GLOBALS, H * SLOTS), 1) % SLOTS
        holds = jnp.where(slot + group * SLOTS == rank, 1.0, 0.0).astype(jnp.bfloat16)
        at = jnp.where(
            rows == lax.broadcasted_iota(jnp.int32, (tok, GLOBALS), 0), 1.0, 0.0
        ).astype(jnp.bfloat16)
        return dot(at, holds).astype(jnp.bfloat16)

    @pl.when(step == 0)
    def _():
        for copy in copies():
            copy.start()

        def fetch(at, count):
            spot = spots[at]
            source = pl.ds(pl.multiple_of(spot // TILE * TILE, TILE), TILE)
            target = pl.ds(pl.multiple_of(at * TILE, TILE), TILE)
            for index, (hbm, tile) in enumerate(((k_hbm, tile_k), (v_hbm, tile_v))):
                pltpu.make_async_copy(
                    hbm.at[source, :], tile.at[target, :], sems.at[2 * (H + 3) + index]
                ).start()
            return count + jnp.where(spot // tok == me, 1, 0)

        owns[0] = lax.fori_loop(0, GLOBALS, fetch, jnp.int32(0))
        for group in range(GLOBALS // SLOTS):

            @pl.when(owns[0] > group * SLOTS)
            def _():
                picked = dot(picker_rows(group), q_ref[...]) * DH ** (-0.5)
                picked = jnp.where(head_mask(picked.shape), picked, 0.0)
                gq[group] = picked.astype(jnp.bfloat16)
                top[group] = jnp.full(top.shape[1:], -1e30, jnp.float32)
                total[group] = jnp.zeros(total.shape[1:], jnp.float32)
                acc[group] = jnp.zeros(acc.shape[1:], jnp.float32)

    for group in range(GLOBALS // SLOTS):

        @pl.when(owns[0] > group * SLOTS)
        def _():
            scores = dot_t(gq[group], kc_ref[...])
            before = top[group]
            peak = jnp.maximum(before, jnp.max(scores, axis=1, keepdims=True))
            scale = jnp.exp(before - peak)
            terms = jnp.exp(scores - peak)
            top[group] = peak
            total[group] = total[group] * scale + jnp.sum(terms, axis=1, keepdims=True)
            acc[group] = acc[group] * scale + dot(terms.astype(jnp.bfloat16), vc_ref[...])

    @pl.when(step == pl.num_programs(0) - 1)
    def _():
        for copy in copies():
            copy.wait()
        for index, (hbm, tile) in enumerate(((k_hbm, tile_k), (v_hbm, tile_v))):
            pltpu.make_async_copy(
                hbm.at[pl.ds(0, GLOBALS * TILE), :], tile, sems.at[2 * (H + 3) + index]
            ).wait()
        spot = lax.broadcasted_iota(jnp.int32, (GLOBALS, GLOBALS * TILE), 1)
        want = lax.broadcasted_iota(jnp.int32, (GLOBALS, GLOBALS * TILE), 0) * TILE
        here = jnp.where(spot == want + column() % TILE, 1.0, 0.0).astype(jnp.bfloat16)
        for pair in range(PAIRS):
            lanes = slice(pair * LANES, (pair + 1) * LANES)
            far_k = join_pair(dil_k[2 * pair], dil_k[2 * pair + 1])
            far_v = join_pair(dil_v[2 * pair], dil_v[2 * pair + 1])
            glob_k = dot(here, tile_k[:, lanes]).astype(jnp.bfloat16)
            glob_v = dot(here, tile_v[:, lanes]).astype(jnp.bfloat16)
            for block in range(tok // BLK):
                rows = slice(block * BLK, (block + 1) * BLK)
                near = slice(block * BLK, (block + 3) * BLK)
                keys = jnp.concatenate([loc_k[near, lanes], far_k[rows], glob_k], axis=0)
                values = jnp.concatenate([loc_v[near, lanes], far_v[rows], glob_v], axis=0)
                scores = dot_t(split_pair(q_ref[rows, lanes]), keys) * DH ** (-0.5)
                terms = jnp.exp(scores - jnp.max(scores, axis=1, keepdims=True))
                weights = terms * (1.0 / jnp.sum(terms, axis=1, keepdims=True))
                mixed = dot(weights.astype(jnp.bfloat16), values)
                mixed = join_pair(mixed[:BLK], mixed[BLK:])
                out_ref[rows, lanes] = mixed.astype(jnp.bfloat16)

        for group in range(GLOBALS // SLOTS):

            @pl.when(owns[0] > group * SLOTS)
            def _():
                ratio = acc[group] / total[group]
                ratio = jnp.where(head_mask(ratio.shape), ratio, 0.0).astype(jnp.bfloat16)
                mine = picker_cols(group)
                placed = dot(mine, ratio).astype(jnp.bfloat16)
                owned = jnp.max(mine.astype(jnp.float32), axis=1, keepdims=True) > 0.5
                out_ref[...] = jnp.where(owned, placed, out_ref[...])


def attention(queries, keys, values, dilation, global_rows):
    tok, width = queries.shape
    length = keys.shape[0]
    groups = GLOBALS // SLOTS
    whole = lambda shape: pl.BlockSpec(shape, lambda i, d, s: (0, 0))
    chunked = pl.BlockSpec((CHUNK, width), lambda i, d, s: (i, 0))
    raw = pl.BlockSpec(memory_space=pl.ANY)
    far = pltpu.VMEM((H, tok, LANES), jnp.bfloat16)
    near = pltpu.VMEM((tok + 2 * BLK, width), jnp.bfloat16)
    tile = pltpu.VMEM((GLOBALS * TILE, width), jnp.bfloat16)
    state = pltpu.VMEM((groups, H * SLOTS, 1), jnp.float32)
    return pl.pallas_call(
        functools.partial(attention_kernel, length),
        out_shape=jax.ShapeDtypeStruct((tok, width), jnp.bfloat16),
        grid_spec=pltpu.PrefetchScalarGridSpec(
            num_scalar_prefetch=2,
            grid=(length // CHUNK,),
            in_specs=[
                whole((tok, width)), whole((1, GLOBALS)),
                chunked, chunked, raw, raw,
            ],
            out_specs=whole((tok, width)),
            scratch_shapes=[
                near, near, far, far, tile, tile,
                pltpu.VMEM((groups, H * SLOTS, width), jnp.bfloat16),
                state, state,
                pltpu.VMEM((groups, H * SLOTS, width), jnp.float32),
                pltpu.SMEM((1,), jnp.int32),
                pltpu.SemaphoreType.DMA((2 * (H + 3) + 2,)),
            ],
        ),
        compiler_params=pltpu.CompilerParams(vmem_limit_bytes=58 << 20),
        cost_estimate=pl.CostEstimate(
            flops=20_000_000_000, bytes_accessed=4 * length * width, transcendentals=5_000_000
        ),
    )(dilation, global_rows, queries, global_rows[None, :], keys, values, keys, values)


MESH = pl.DeviceIdType.MESH


def gather_kernel(chips, *refs):
    ins, outs, sems = refs[:4], refs[4:8], refs[8:]
    ring_send, ring_recv, pair_send, pair_recv, core_send, core_recv, own_sems = sems
    half = chips // 2
    group, seq = lax.axis_index("group"), lax.axis_index("seq")
    role = group % 2
    chip, core = seq // 2, seq % 2
    odd = chip % 2
    pos = (1 - odd) * (chip // 2) + odd * (chips - 1 - chip // 2)

    def chip_at(place):
        place = (place + 2 * chips) % chips
        late = place // half
        return (1 - late) * 2 * place + late * (2 * (chips - 1 - place) + 1)

    ahead = (group, chip_at(pos + 1) * 2 + core)
    behind = (group, chip_at(pos - 1) * 2 + core)
    beside = (group, chip * 2 + 1 - core)
    across = (group + 1 - 2 * role, seq)

    barrier = pltpu.get_barrier_semaphore()
    for other in (ahead, behind, beside, across):
        pl.semaphore_signal(barrier, inc=1, device_id=other, device_id_type=MESH)
    pl.semaphore_wait(barrier, 4)

    def columns(at, side, part):
        width = ins[at].shape[1]
        first = 0
        if at < 2 and side is not None:
            width = width // 2
            first = side * width
        if part is not None:
            width = width // 2
            first = first + part * width
        if isinstance(first, int):
            return pl.ds(first, width)
        return pl.ds(pl.multiple_of(first, 128), width)

    def held(at, place, side, part):
        rows = ins[at].shape[0]
        first = (chip_at(place) * 2 + core) * rows
        return outs[at].at[pl.ds(pl.multiple_of(first, 8), rows), columns(at, side, part)]

    def twin(at, place, side, part):
        rows = ins[at].shape[0]
        first = (chip_at(place) * 2 + 1 - core) * rows
        return outs[at].at[pl.ds(pl.multiple_of(first, 8), rows), columns(at, side, part)]

    def part_of(way, hop):
        return way if hop == half else None

    def sign(way):
        return 1 - 2 * way

    def remote(source, target, send, recv, other):
        return pltpu.make_async_remote_copy(
            src_ref=source, dst_ref=target, send_sem=send, recv_sem=recv,
            device_id=other, device_id_type=MESH,
        )

    sent = []

    def ring(at, way, hop):
        index = (at * 2 + way) * half + hop - 1
        return ring_send.at[index], ring_recv.at[index], (ahead, behind)[way]

    def ring_start(at, way, hop):
        place, part = pos - sign(way) * (hop - 1), part_of(way, hop)
        target = held(at, place, role, part)
        source = ins[at].at[:, columns(at, role, part)] if hop == 1 else target
        copy = remote(source, target, *ring(at, way, hop))
        copy.start()
        sent.append(copy)

    def ring_wait(at, way, hop):
        here = held(at, pos - sign(way) * hop, role, part_of(way, hop))
        remote(here, here, *ring(at, way, hop)).wait_recv()

    def pair(at, way, hop):
        index = (at * 2 + way) * half + hop - 1
        return pair_send.at[index], pair_recv.at[index], across

    def pair_start(at, way, hop):
        here = held(at, pos - sign(way) * hop, role, part_of(way, hop))
        copy = remote(here, here, *pair(at, way, hop))
        copy.start()
        sent.append(copy)

    def pair_wait(at, way, hop):
        here = held(at, pos - sign(way) * hop, 1 - role, part_of(way, hop))
        remote(here, here, *pair(at, way, hop)).wait_recv()

    passed = []

    def core_start(at, place, side, part, source=None):
        index = len(passed)
        target = held(at, place, side, part)
        copy = remote(
            target if source is None else source, target,
            core_send.at[index], core_recv.at[index], beside,
        )
        copy.start()
        sent.append(copy)
        passed.append((at, place, side, part))

    own = []
    for at in (0, 1):
        for way in range(2):
            ring_start(at, way, 1)
    for at in range(4):
        core_start(at, pos, None, None, ins[at])
        copy = pltpu.make_async_copy(ins[at], held(at, pos, None, None), own_sems.at[at])
        copy.start()
        own.append(copy)

    def ring_step(at, hop):
        for way in range(2):
            ring_wait(at, way, hop)
            if hop < half:
                ring_start(at, way, hop + 1)
            if at < 2:
                pair_start(at, way, hop)
            core_start(at, pos - sign(way) * hop, role, part_of(way, hop))

    for hop in range(1, half + 2):
        if hop <= half:
            ring_step(0, hop)
            ring_step(1, hop)
        if hop == 1:
            for at in (2, 3):
                for way in range(2):
                    ring_start(at, way, 1)
        if hop > 1:
            ring_step(2, hop - 1)
            ring_step(3, hop - 1)
            for at in range(2):
                for way in range(2):
                    pair_wait(at, way, hop - 1)
                    core_start(at, pos - sign(way) * (hop - 1), 1 - role, part_of(way, hop - 1))
    for index, (at, place, side, part) in enumerate(passed):
        here = twin(at, place, side, part)
        remote(here, here, core_send.at[index], core_recv.at[index], beside).wait_recv()
    for copy in sent:
        copy.wait_send()
    for copy in own:
        copy.wait()


def gathered(arrays):
    devices = lax.axis_size("seq")
    chips = devices // 2
    half = chips // 2
    raw = pl.BlockSpec(memory_space=pl.ANY)
    dma = pltpu.SemaphoreType.DMA
    return pl.pallas_call(
        functools.partial(gather_kernel, chips),
        out_shape=[
            jax.ShapeDtypeStruct((a.shape[0] * devices, a.shape[1]), a.dtype) for a in arrays
        ],
        in_specs=[raw] * 4,
        out_specs=[raw] * 4,
        scratch_shapes=[
            dma((8 * half,)), dma((8 * half,)), dma((4 * half,)), dma((4 * half,)),
            dma((4 + 12 * half,)), dma((4 + 12 * half,)), dma((4,)),
        ],
        compiler_params=pltpu.CompilerParams(collective_id=0, has_side_effects=True),
    )(*arrays)


def per_device(queries, key_rows, value_rows, dilation, global_rows, out_weight, mlp_up, mlp_down):
    up, down, keys, values = gathered((mlp_up, mlp_down, key_rows, value_rows))
    mixed = attention(queries, keys, values, dilation, global_rows)
    attended = jnp.dot(mixed, out_weight, preferred_element_type=jnp.float32).astype(jnp.bfloat16)
    pre_act = jnp.dot(attended, up, preferred_element_type=jnp.float32)
    hidden = jax.nn.gelu(pre_act, approximate=True).astype(jnp.bfloat16)
    mlp_out = jnp.dot(hidden, down, preferred_element_type=jnp.float32).astype(jnp.bfloat16)
    return attended, mlp_out


def solution(mesh):
    rows = P(("group", "seq"), None)
    return jax.shard_map(
        per_device,
        mesh=mesh,
        in_specs=(rows, rows, rows, P(), P("group"), P(), P("seq", None), P("seq", None)),
        out_specs=(rows, rows),
        check_vma=False,
    )
```
